32 devices in a mesh: replica: 8 (over z, y), domain: 4 (over x, core).
Axes of the slice: x: 2, y: 2, z: 4, core: 2. Of those that a mesh axis runs over, the one named last changes fastest.
Arguments:
- particle_coordinates: float32 [8, 3, 32768], P('replica', None, 'domain'), may hold values from 0 to 8, as said below
- particle_speeds: float32 [8, 3, 32768], P('replica', None, 'domain'), may hold values from -6 to 6
- point_charge_values: float32 [32768], P('domain'), may hold values from -1 to 1
- reciprocal_weights: float32 [32768], P('domain'), may hold values from 0.5 to 2
- wiener_increments: float32 [8, 4, 3, 32768], P('replica', None, None, 'domain'), may hold values from -6 to 6
- heat_levels: float32 [8], P('replica'), may hold values from 0.5 to 2
- neighbour_group_table: int32 [8, 4096, 8], P('replica', 'domain'), may hold values from 0 to 2559
- neighbour_group_tally: int32 [8, 4096], P('replica', 'domain'), may hold values from 4 to 8
- loaned_group_slots: int32 [8, 2, 3072], P('replica', None, 'domain'), may hold values from 0 to 1023
- swap_mate: int32 [8], replicated, may hold values from 0 to 7, as said below
Outputs:
- positions_out: float32 [8, 3, 32768], P('replica', None, 'domain')
- velocities_out: float32 [8, 3, 32768], P('replica', None, 'domain')
- forces_out: float32 [8, 3, 32768], P('replica', None, 'domain')
- potential_per_particle: float32 [8], P('replica')
- exchange_delta: float32 [8], P('replica')
The draws below stay inside these ranges and needn't reach their ends.
Inputs may be any that keep to these rules, and one draw needn't show every extreme that they name: `particle_coordinates`: the first coordinate of an atom of slab d lies in [2 d, 2 d + 2); the other two lie in [0, 3). Partner pairs the replicas: swap_mate[swap_mate[r]] = r and swap_mate[r] != r.
All inputs are finite; a program needn't handle non-finite values.
Results may differ from the reference program's by a relative error of at most 0.0003.
Values sent between devices are 32-bit elements; how exact they have to be, the bound alone decides.
A program may use at most 64 MiB of HBM per device.

```python
import math
import jax
import jax.numpy as jnp
from jax import lax

CLS = 8
CLUSTERS_DEV = 1024
NP = 8
STEPS = 4
HALO_CL = 768
EXT = 2560
DOMAINS = 4
LADDER_RUNGS = 8
ATOMS_DEV = 8192
ATOMS = 32768
CLUSTERS = 4096


SLAB_LEN = 2.0


SIDE_LOW = 1.5


SIDE_SPAN = 1.5


def draw_particle_coordinates(key, part):
    unit = jax.random.uniform(jax.random.fold_in(key, 11), (LADDER_RUNGS, 3, ATOMS), jnp.float32)
    sides = SIDE_LOW + SIDE_SPAN * jax.random.uniform(jax.random.fold_in(key, 23), (LADDER_RUNGS,), jnp.float32)
    slab = (jnp.arange(ATOMS) // ATOMS_DEV).astype(jnp.float32)
    first = (slab[None, :] + unit[:, 0]) * SLAB_LEN
    return jnp.stack([first, unit[:, 1] * sides[:, None], unit[:, 2] * sides[:, None]], axis=1)


def draw_swap_mate(key, part):
    order = jax.random.permutation(key, LADDER_RUNGS).astype(jnp.int32)
    first = order[0::2]
    second = order[1::2]
    result = jnp.zeros((LADDER_RUNGS,), jnp.int32)
    return result.at[first].set(second).at[second].set(first)


def plant(values, rng, low, high):
    shape = values.shape
    index_at = [jax.random.randint(jax.random.fold_in(rng, axis), (), 0, shape[axis]) for axis in range(len(shape))]
    values = values.at[tuple(index_at)].set(low)
    longest = shape.index(max(shape))
    index_at[longest] = (index_at[longest] + 1) % shape[longest]
    return values.at[tuple(index_at)].set(high)


def levels(stream_key, extent, cuts, least, largest):
    gain = 1.0
    for axis_at, shards_of in cuts:
        draws = jax.random.uniform(jax.random.fold_in(jax.random.fold_in(stream_key, 6), axis_at), (shards_of,), jnp.float32, least / len(cuts), largest / len(cuts))
        gain = gain * jnp.repeat(jnp.exp(draws), extent[axis_at] // shards_of).reshape((-1,) + (1,) * (len(extent) - 1 - axis_at))
    return gain


def normal_values(own_key, shape, scale, bound, shards=(), kind=jnp.bfloat16):
    values = scale * jax.random.normal(own_key, shape, jnp.float32)
    if shards:
        values = values * levels(own_key, shape, shards, -0.22, 0.18)
    return jnp.clip(values, -bound, bound).astype(kind)


def setup_inputs(seed: int = 0) -> dict:
    key_of = jax.random.split(jax.random.key(seed), 11)
    return {
        "particle_coordinates": draw_particle_coordinates(jax.random.fold_in(key_of[10], 71), 0),
        "particle_speeds": normal_values(key_of[1], (LADDER_RUNGS, 3, ATOMS), 1.0, 6.0, ((0, 8), (2, 4)), jnp.float32),
        "point_charge_values": jnp.clip(jax.random.uniform(key_of[2], (ATOMS,), jnp.float32, -1.0, 1.0) * levels(key_of[2], (ATOMS,), ((0, 4),), -0.4, 0.0), -1.0, 1.0),
        "reciprocal_weights": jnp.clip(jnp.exp(math.log(2.0) - 1.3862944 * jax.random.uniform(key_of[3], (ATOMS,), jnp.float32) ** levels(key_of[3], (ATOMS,), ((0, 4),), -0.2, 0.2)), 0.5, 2.0),
        "wiener_increments": normal_values(key_of[4], (LADDER_RUNGS, STEPS, 3, ATOMS), 1.0, 6.0, ((0, 8), (3, 4)), jnp.float32),
        "heat_levels": jnp.clip(jnp.exp(math.log(2.0) - 1.3862944 * jax.random.uniform(key_of[5], (LADDER_RUNGS,), jnp.float32) ** levels(key_of[5], (LADDER_RUNGS,), ((0, 8),), -0.2, 0.2)), 0.5, 2.0),
        "neighbour_group_table": plant(jax.random.randint(key_of[6], (LADDER_RUNGS, CLUSTERS, NP), 0, EXT), jax.random.fold_in(key_of[6], 1), 0, EXT - 1).astype(jnp.int32),
        "neighbour_group_tally": plant(jax.random.randint(key_of[7], (LADDER_RUNGS, CLUSTERS), NP // 2, NP + 1), jax.random.fold_in(key_of[7], 1), NP // 2, NP).astype(jnp.int32),
        "loaned_group_slots": plant(jax.random.randint(key_of[8], (LADDER_RUNGS, 2, HALO_CL * DOMAINS), 0, CLUSTERS_DEV), jax.random.fold_in(key_of[8], 1), 0, CLUSTERS_DEV - 1).astype(jnp.int32),
        "swap_mate": draw_swap_mate(jax.random.fold_in(key_of[10], 71), 0),
    }


SLAB_LEN = 2.0
CUT_SQ = 9.0
SOFT_CORE = 1.0
FIELD_TERM = 1.0 / 54.0
HALF_STEP = 0.05
FRICTION_DECAY = math.exp(-0.5)
NOISE_SCALE = math.sqrt(1.0 - math.exp(-1.0))

def pair_terms(own, part, plist, counts, first):
    diff = own[:3, :, None, None, :] - part[:3, None, :, :, :]
    dist_sq = lax.optimization_barrier(jnp.sum(diff * diff, axis=0))
    shifted = dist_sq + SOFT_CORE
    inv_s = 1.0 / shifted
    inv_three = inv_s * inv_s * inv_s
    inv_six = inv_three * inv_three
    dispersion = inv_six - inv_three
    dispersion_slope = -6.0 * inv_six * inv_s + 3.0 * inv_three * inv_s
    charges = own[3][:, None, None, :] * part[3][None]
    root = lax.rsqrt(shifted)
    coulomb = charges * (root + FIELD_TERM * dist_sq)
    coulomb_slope = charges * (-0.5 * root * inv_s + FIELD_TERM)
    taper_base = jnp.maximum(1.0 - dist_sq / CUT_SQ, 0.0)
    potential = dispersion + coulomb
    slot = lax.broadcasted_iota(jnp.int32, (1, 1, plist.shape[0], 1), 2)
    live = slot < counts[None, None, None, :]
    own_index = first + lax.broadcasted_iota(jnp.int32, (1, 1, 1, plist.shape[1]), 3)
    same_atom = lax.broadcasted_iota(jnp.int32, (own.shape[1], own.shape[1], 1, 1), 0) == lax.broadcasted_iota(jnp.int32, (own.shape[1], own.shape[1], 1, 1), 1)
    is_self = (plist[None, None] == own_index) & same_atom
    weight = jnp.where(live & jnp.logical_not(is_self), 1.0, 0.0).astype(jnp.float32)
    potential_per_particle = 0.5 * jnp.sum(weight * potential * taper_base * taper_base)
    slope = weight * ((dispersion_slope + coulomb_slope) * taper_base * taper_base - 2.0 / CUT_SQ * potential * taper_base)
    force = -2.0 * lax.optimization_barrier(jnp.sum(slope[None] * diff, axis=(2, 3)))
    return (force, potential_per_particle)

def local_forces(extended, plist, counts):
    clusters = plist.shape[0]
    partners = plist.shape[1]
    width = extended.shape[2]
    block = math.gcd(clusters, 512)
    blocks = clusters // block
    ext_t = jnp.transpose(extended, (0, 2, 1))
    own_blocks = ext_t[:, :, :clusters].reshape(4, width, blocks, block).transpose(2, 0, 1, 3)
    plist_blocks = plist.reshape(blocks, block, partners).transpose(0, 2, 1)
    count_blocks = counts.reshape(blocks, block)
    firsts = (jnp.arange(blocks) * block).astype(jnp.int32)

    def one_block(items):
        own_b, plist_b, count_b, first = items
        part = jnp.take(ext_t, plist_b, axis=2)
        return pair_terms(own_b, part, plist_b, count_b, first)
    forces, energies = lax.map(one_block, (own_blocks, plist_blocks, count_blocks, firsts))
    forces = forces.transpose(1, 0, 3, 2).reshape(3, clusters * width)
    return (forces, jnp.sum(energies))

def reference(particle_coordinates, particle_speeds, point_charge_values, reciprocal_weights, wiener_increments, heat_levels, neighbour_group_table, neighbour_group_tally, loaned_group_slots, swap_mate):
    reps = particle_coordinates.shape[0]
    atoms = particle_coordinates.shape[2]
    domains = DOMAINS
    clusters = CLUSTERS_DEV
    width = CLS
    lent = HALO_CL
    box = SLAB_LEN * domains
    plist = neighbour_group_table.reshape(reps * domains, clusters, NP)
    counts = neighbour_group_tally.reshape(reps * domains, clusters)
    halo = loaned_group_slots.reshape(reps, 2, domains, lent)
    charge_rows = jnp.broadcast_to(point_charge_values.reshape(1, 1, domains, clusters, width), (reps, 1, domains, clusters, width))
    domain_ids = jnp.arange(domains)
    prev_shift = jnp.where(domain_ids == 0, -box, 0.0).astype(jnp.float32)
    next_shift = jnp.where(domain_ids == domains - 1, box, 0.0).astype(jnp.float32)
    row_mask = jnp.array([1.0, 0.0, 0.0, 0.0], dtype=jnp.float32)
    index_next = jnp.broadcast_to(halo[:, 0][:, None, :, :, None], (reps, 4, domains, lent, width))
    index_prev = jnp.broadcast_to(halo[:, 1][:, None, :, :, None], (reps, 4, domains, lent, width))

    def evaluate(coords):
        payload = jnp.concatenate([coords.reshape(reps, 3, domains, clusters, width), charge_rows], axis=1)
        send_next = jnp.take_along_axis(payload, index_next, axis=3)
        send_prev = jnp.take_along_axis(payload, index_prev, axis=3)
        from_prev = jnp.roll(send_next, 1, axis=2) + prev_shift[None, None, :, None, None] * row_mask[None, :, None, None, None]
        from_next = jnp.roll(send_prev, -1, axis=2) + next_shift[None, None, :, None, None] * row_mask[None, :, None, None, None]
        extended = jnp.concatenate([payload, from_prev, from_next], axis=3)
        extended = extended.transpose(0, 2, 1, 3, 4).reshape(reps * domains, 4, clusters + 2 * lent, width)
        forces, energies = lax.map(lambda items: local_forces(items[0], items[1], items[2]), (extended, plist, counts))
        forces = forces.reshape(reps, domains, 3, clusters * width).transpose(0, 2, 1, 3).reshape(reps, 3, atoms)
        return (forces, energies.reshape(reps, domains))
    reciprocal_particle_weight = reciprocal_weights[None, None, :]
    reciprocal_heat_gap = jnp.sqrt(heat_levels[:, None, None] * reciprocal_particle_weight)
    coords = particle_coordinates
    vel = particle_speeds
    force, energies = evaluate(coords)
    for step in range(STEPS):
        vel = vel + HALF_STEP * reciprocal_particle_weight * force
        coords = coords + HALF_STEP * vel
        vel = FRICTION_DECAY * vel + NOISE_SCALE * reciprocal_heat_gap * wiener_increments[:, step]
        coords = coords + HALF_STEP * vel
        force, energies = evaluate(coords)
        vel = vel + HALF_STEP * reciprocal_particle_weight * force
    potential_per_particle = lax.optimization_barrier(jnp.sum(energies, axis=1)) / atoms
    potential_gap = (1.0 / heat_levels - 1.0 / heat_levels[swap_mate]) * (potential_per_particle - potential_per_particle[swap_mate])
    return (coords, vel, force, potential_per_particle, potential_gap)
```

```python
import functools
import math

import jax
import jax.numpy as jnp
from jax import lax
from jax.experimental import pallas as pl
from jax.experimental.pallas import tpu as pltpu
from jax.sharding import PartitionSpec as P

SLAB_LEN = 2.0
CUT_SQ = 9.0
FIELD_TERM = 1.0 / 54.0
HALF_STEP = 0.05
FRICTION_DECAY = math.exp(-0.5)
NOISE_SCALE = math.sqrt(1.0 - math.exp(-1.0))
FAR = 1.0e6
MESH = pl.DeviceIdType.MESH
L = 128
W = 8


def picked(x, lane):
    return jnp.take_along_axis(x, lane, axis=1, mode="promise_in_bounds")


def fori(n, body):
    def step(i, c):
        body(i)
        return c

    lax.fori_loop(0, n, step, 0)


def wide(row):
    return jnp.broadcast_to(row, (W, L))


def kernel(
    replicas,
    domains,
    x_in,
    v_in,
    q_in,
    m_in,
    w_in,
    heat,
    plist_in,
    tally_in,
    loan_in,
    mate,
    x_out,
    v_out,
    f_out,
    pot_out,
    gap_out,
    own,
    halo,
    sbuf,
    qown,
    qhalo,
    qsend,
    vel,
    frc,
    rows,
    hm,
    nzc,
    noise,
    lane_ref,
    chunk_ref,
    self_ref,
    slane,
    schunk,
    part,
    qpart,
    eacc,
    epack,
    ebuf,
    rpack,
    rbuf,
    send_sem,
    recv_sem,
    qsend_sem,
    qrecv_sem,
    esend_sem,
    erecv_sem,
    rsend_sem,
    rrecv_sem,
):
    groups = own.shape[0]
    lent = sbuf.shape[2]
    partners = lane_ref.shape[1]
    steps = w_in.shape[1]
    me_r = lax.axis_index("replica")
    me_d = lax.axis_index("domain")
    nxt = lax.rem(me_d + 1, domains)
    prv = lax.rem(me_d + domains - 1, domains)
    box = SLAB_LEN * domains

    barrier = pltpu.get_barrier_semaphore()
    for o in range(1, domains):
        pl.semaphore_signal(
            barrier, inc=1, device_id=(me_r, lax.rem(me_d + o, domains)), device_id_type=MESH
        )
    for o in range(1, replicas):
        pl.semaphore_signal(
            barrier, inc=1, device_id=(lax.rem(me_r + o, replicas), me_d), device_id_type=MESH
        )

    sub_iota = lax.broadcasted_iota(jnp.int32, (W, L), 0)
    lane_iota = lax.broadcasted_iota(jnp.int32, (W, L), 1)
    in_lane = (lane_iota & 15) * W + sub_iota
    in_row = lane_iota >> 4
    out_lane = sub_iota * 16 + (lane_iota >> 3)
    out_row = lane_iota & 7

    def pack(row_of):
        acc = picked(wide(row_of(0)), in_lane)
        for r in range(1, W):
            acc = jnp.where(in_row == r, picked(wide(row_of(r)), in_lane), acc)
        return acc

    def unpack(ref, g, base):
        acc = picked(wide(ref[g, pl.ds(base, 1), :]), out_lane)
        for r in range(1, W):
            acc = jnp.where(out_row == r, picked(wide(ref[g, pl.ds(base + r, 1), :]), out_lane), acc)
        return acc

    kt = heat[0]

    def setup_coords(g):
        def at(r):
            return pl.ds(pl.multiple_of((g * W + r) * L, L), L)

        for f in range(3):
            own[g, f * W : (f + 1) * W, :] = pack(lambda r: x_in[0, f : f + 1, at(r)])
        qown[g] = pack(lambda r: q_in[pl.ds(g * W + r, 1), :])

    fori(groups, setup_coords)

    def setup_loan(h):
        at = pl.ds(pl.multiple_of(h * L, L), L)
        for s in range(2):
            p = wide(loan_in[0, s : s + 1, at])
            slane[s, h] = p & (L - 1)
            schunk[s, h] = p >> 7

    fori(lent, setup_loan)

    def fill_send(s, slot):
        shift = jnp.where(
            me_d == (domains - 1 if s == 0 else 0), -box if s == 0 else box, 0.0
        ).astype(jnp.float32)

        def one(h):
            lane, chunk = slane[s, h], schunk[s, h]
            acc = [picked(own[0, f * W : (f + 1) * W, :], lane) for f in range(3)]
            for j in range(1, groups):
                hit = chunk == j
                for f in range(3):
                    acc[f] = jnp.where(hit, picked(own[j, f * W : (f + 1) * W, :], lane), acc[f])
            acc[0] = acc[0] + shift
            for f in range(3):
                sbuf[slot, s, h, f * W : (f + 1) * W, :] = acc[f]

        fori(lent, one)

    def halo_copy(s, slot):
        return pltpu.make_async_remote_copy(
            src_ref=sbuf.at[slot, s],
            dst_ref=halo.at[slot, s],
            send_sem=send_sem.at[slot, s],
            recv_sem=recv_sem.at[slot, s],
            device_id=(me_r, nxt if s == 0 else prv),
            device_id_type=MESH,
        )

    def charge_copy(s):
        return pltpu.make_async_remote_copy(
            src_ref=qsend.at[s],
            dst_ref=qhalo.at[s],
            send_sem=qsend_sem.at[s],
            recv_sem=qrecv_sem.at[s],
            device_id=(me_r, nxt if s == 0 else prv),
            device_id_type=MESH,
        )

    def fill_charges(h):
        for s in range(2):
            lane, chunk = slane[s, h], schunk[s, h]
            acc = picked(qown[0], lane)
            for j in range(1, groups):
                acc = jnp.where(chunk == j, picked(qown[j], lane), acc)
            qsend[s, h] = acc

    fori(lent, fill_charges)
    pl.semaphore_wait(barrier, domains - 1 + replicas - 1)
    for s in range(2):
        charge_copy(s).start()

    def setup_lists(g):
        at = pl.ds(pl.multiple_of(g * L, L), L)
        p = plist_in[0, at, :].T
        live = lax.broadcasted_iota(jnp.int32, p.shape, 0) < tally_in[0:1, at]
        lane_ref[g] = p & (L - 1)
        chunk_ref[g] = jnp.where(live, p >> 7, -1)
        here = g * L + lax.broadcasted_iota(jnp.int32, p.shape, 1)
        self_ref[g] = (p == here).astype(jnp.int32)

    fori(groups, setup_lists)

    def setup_rest(g):
        def at(r):
            return pl.ds(pl.multiple_of((g * W + r) * L, L), L)

        for f in range(3):
            vel[g, f * W : (f + 1) * W, :] = pack(lambda r: v_in[0, f : f + 1, at(r)])
        m = pack(lambda r: m_in[pl.ds(g * W + r, 1), :])
        hm[g] = HALF_STEP * m
        nzc[g] = NOISE_SCALE * jnp.sqrt(kt * m)

    def setup_noise(n):
        def one(g):
            def at(r):
                return pl.ds(pl.multiple_of((g * W + r) * L, L), L)

            for f in range(3):
                noise[g, f * W : (f + 1) * W, :] = pack(lambda r: w_in[0, n, f : f + 1, at(r)])

        fori(groups, one)

    def charges_near(g):
        for k in range(partners):
            lane, chunk = wide(lane_ref[g, k : k + 1, :]), wide(chunk_ref[g, k : k + 1, :])
            acc = jnp.zeros((W, L), jnp.float32)
            for j in range(groups):
                acc = jnp.where(chunk == j, picked(qown[j], lane), acc)
            qpart[g, k] = acc

    def charges_far(g):
        for k in range(partners):
            lane, chunk = wide(lane_ref[g, k : k + 1, :]), wide(chunk_ref[g, k : k + 1, :])
            acc = qpart[g, k]
            for s in range(2):
                for j in range(lent):
                    hit = chunk == groups + s * lent + j
                    acc = jnp.where(hit, picked(qhalo[s, j], lane), acc)
            qpart[g, k] = acc

    def near(g):
        for k in range(partners):
            lane, chunk = wide(lane_ref[g, k : k + 1, :]), wide(chunk_ref[g, k : k + 1, :])
            acc = [jnp.full((W, L), FAR, jnp.float32)] * 3
            for j in range(groups):
                hit = chunk == j
                for f in range(3):
                    acc[f] = jnp.where(hit, picked(own[j, f * W : (f + 1) * W, :], lane), acc[f])
            for f in range(3):
                part[g, k, f * W : (f + 1) * W, :] = acc[f]

    def far(g, slot):
        for k in range(partners):
            lane, chunk = wide(lane_ref[g, k : k + 1, :]), wide(chunk_ref[g, k : k + 1, :])
            acc = [part[g, k, f * W : (f + 1) * W, :] for f in range(3)]
            for s in range(2):
                for j in range(lent):
                    hit = chunk == groups + s * lent + j
                    for f in range(3):
                        acc[f] = jnp.where(
                            hit, picked(halo[slot, s, j, f * W : (f + 1) * W, :], lane), acc[f]
                        )
            for f in range(3):
                part[g, k, f * W : (f + 1) * W, :] = acc[f]

    def pairs(g, with_energy):
        def one_atom(i):
            mine = [wide(own[g, pl.ds(f * W + i, 1), :]) for f in range(3)]
            my_q = wide(qown[g, pl.ds(i, 1), :])
            acc = [jnp.zeros((W, L), jnp.float32)] * 3
            energy = jnp.zeros((W, L), jnp.float32)
            for k in range(partners):
                d = [mine[f] - part[g, k, f * W : (f + 1) * W, :] for f in range(3)]
                t = d[0] * d[0] + d[1] * d[1] + d[2] * d[2]
                root = lax.rsqrt(t + 1.0)
                inv = root * root
                inv3 = inv * inv * inv
                q = my_q * qpart[g, k]
                w = jnp.maximum(1.0 - t * (1.0 / CUT_SQ), 0.0)
                u = inv3 * (inv3 - 1.0) + q * (root + FIELD_TERM * t)
                du = inv * inv3 * (3.0 - 6.0 * inv3) + q * (FIELD_TERM - 0.5 * (root * inv))
                slope = w * (du * w - (2.0 / CUT_SQ) * u)
                for f in range(3):
                    acc[f] = acc[f] + slope * d[f]
                if with_energy:
                    same = (sub_iota == i) & (wide(self_ref[g, k : k + 1, :]) == 1)
                    energy = energy + jnp.where(same, 0.0, u * (w * w))
            for f in range(3):
                rows[pl.ds(f * W + i, 1), :] = -2.0 * jnp.sum(acc[f], axis=0, keepdims=True)
            if with_energy:
                eacc[...] += energy

        fori(W, one_atom)

    def exchange_start(slot):
        for s in range(2):
            fill_send(s, slot)
            halo_copy(s, slot).start()

    def exchange_wait(slot):
        for s in range(2):
            halo_copy(s, slot).wait()

    def step(n):
        slot = lax.rem(n, 2)
        exchange_start(slot)
        fori(groups, near)
        setup_noise(n)
        exchange_wait(slot)
        kick = jnp.where(n == 0, 1.0, 2.0).astype(jnp.float32)

        def one(g):
            far(g, slot)
            pairs(g, False)
            for f in range(3):
                at = slice(f * W, (f + 1) * W)
                v = vel[g, at, :] + kick * (hm[g] * rows[at, :])
                x = own[g, at, :] + HALF_STEP * v
                v = FRICTION_DECAY * v + nzc[g] * noise[g, at, :]
                vel[g, at, :] = v
                own[g, at, :] = x + HALF_STEP * v

        fori(groups, one)

    fori(groups, setup_rest)
    fori(groups, charges_near)
    for s in range(2):
        charge_copy(s).wait()
    fori(groups, charges_far)
    fori(steps, step)

    last = steps % 2
    exchange_start(last)
    fori(groups, near)

    def store_out(g, ref, base_of, out):
        for f in range(3):
            val = unpack(ref, g, f * W)
            for r in range(W):
                at = pl.ds(pl.multiple_of((g * W + r) * L, L), L)
                out[0, f : f + 1, at] = val[r : r + 1, :]

    fori(groups, lambda g: store_out(g, own, 0, x_out))
    exchange_wait(last)
    eacc[...] = jnp.zeros_like(eacc)

    def final(g):
        far(g, last)
        pairs(g, True)
        for f in range(3):
            at = slice(f * W, (f + 1) * W)
            frc[g, at, :] = rows[at, :]
            vel[g, at, :] = vel[g, at, :] + hm[g] * rows[at, :]

    fori(groups, final)

    epack[...] = jnp.full(epack.shape, 0.5 * jnp.sum(eacc[...]), jnp.float32)

    def energy_copy(o):
        return pltpu.make_async_remote_copy(
            src_ref=epack,
            dst_ref=ebuf.at[me_d],
            send_sem=esend_sem.at[o],
            recv_sem=erecv_sem.at[o],
            device_id=(me_r, lax.rem(me_d + o, domains)),
            device_id_type=MESH,
        )

    for o in range(1, domains):
        energy_copy(o).start()
    ebuf[me_d] = epack[...]
    fori(groups, lambda g: store_out(g, frc, 0, f_out))
    for o in range(1, domains):
        energy_copy(o).wait()
    total = ebuf[0]
    for d in range(1, domains):
        total = total + ebuf[d]
    per_atom = total / float(groups * L * W * domains)
    packet_lane = lax.broadcasted_iota(jnp.int32, per_atom.shape, 1)
    rpack[...] = jnp.where(packet_lane == 0, per_atom, kt)

    def rung_copy(o):
        return pltpu.make_async_remote_copy(
            src_ref=rpack,
            dst_ref=rbuf.at[me_r],
            send_sem=rsend_sem.at[o],
            recv_sem=rrecv_sem.at[o],
            device_id=(lax.rem(me_r + o, replicas), me_d),
            device_id_type=MESH,
        )

    for o in range(1, replicas):
        rung_copy(o).start()
    rbuf[me_r] = rpack[...]
    fori(groups, lambda g: store_out(g, vel, 0, v_out))
    for o in range(1, replicas):
        rung_copy(o).wait()
    partner = mate[0]
    for r in range(1, replicas):
        partner = jnp.where(me_r == r, mate[r], partner)
    other = rbuf[0]
    for r in range(1, replicas):
        other = jnp.where(partner == r, rbuf[r], other)
    other_e = jnp.sum(jnp.where(packet_lane == 0, other, 0.0))
    other_t = jnp.sum(jnp.where(packet_lane == 1, other, 0.0))
    gap = (1.0 / jnp.full_like(per_atom, kt) - 1.0 / jnp.full_like(per_atom, other_t)) * (
        per_atom - other_e
    )
    pot_out[...] = per_atom
    gap_out[...] = gap


def on_device(x, v, q, m, w, heat, plist, tally, loan, mate):
    replicas = lax.axis_size("replica")
    domains = lax.axis_size("domain")
    clusters, partners = plist.shape[1:]
    groups = clusters // L
    lent = loan.shape[2] // L
    f32, i32 = jnp.float32, jnp.int32
    vmem = pl.BlockSpec(memory_space=pltpu.VMEM)
    smem = pl.BlockSpec(memory_space=pltpu.SMEM)
    out = pl.pallas_call(
        functools.partial(kernel, replicas, domains),
        name="langevin",
        out_shape=(
            jax.ShapeDtypeStruct(x.shape, f32),
            jax.ShapeDtypeStruct(x.shape, f32),
            jax.ShapeDtypeStruct(x.shape, f32),
            jax.ShapeDtypeStruct((1, L), f32),
            jax.ShapeDtypeStruct((1, L), f32),
        ),
        in_specs=[vmem, vmem, vmem, vmem, vmem, smem, vmem, vmem, vmem, smem],
        out_specs=(vmem,) * 5,
        scratch_shapes=[
            pltpu.VMEM((groups, 3 * W, L), f32),
            pltpu.VMEM((2, 2, lent, 3 * W, L), f32),
            pltpu.VMEM((2, 2, lent, 3 * W, L), f32),
            pltpu.VMEM((groups, W, L), f32),
            pltpu.VMEM((2, lent, W, L), f32),
            pltpu.VMEM((2, lent, W, L), f32),
            pltpu.VMEM((groups, 3 * W, L), f32),
            pltpu.VMEM((groups, 3 * W, L), f32),
            pltpu.VMEM((3 * W, L), f32),
            pltpu.VMEM((groups, W, L), f32),
            pltpu.VMEM((groups, W, L), f32),
            pltpu.VMEM((groups, 3 * W, L), f32),
            pltpu.VMEM((groups, partners, L), i32),
            pltpu.VMEM((groups, partners, L), i32),
            pltpu.VMEM((groups, partners, L), i32),
            pltpu.VMEM((2, lent, W, L), i32),
            pltpu.VMEM((2, lent, W, L), i32),
            pltpu.VMEM((groups, partners, 3 * W, L), f32),
            pltpu.VMEM((groups, partners, W, L), f32),
            pltpu.VMEM((W, L), f32),
            pltpu.VMEM((1, L), f32),
            pltpu.VMEM((domains, 1, L), f32),
            pltpu.VMEM((1, L), f32),
            pltpu.VMEM((replicas, 1, L), f32),
            pltpu.SemaphoreType.DMA((2, 2)),
            pltpu.SemaphoreType.DMA((2, 2)),
            pltpu.SemaphoreType.DMA((2,)),
            pltpu.SemaphoreType.DMA((2,)),
            pltpu.SemaphoreType.DMA((domains,)),
            pltpu.SemaphoreType.DMA((domains,)),
            pltpu.SemaphoreType.DMA((replicas,)),
            pltpu.SemaphoreType.DMA((replicas,)),
        ],
        compiler_params=pltpu.CompilerParams(collective_id=0, has_side_effects=True),
    )(
        x,
        v,
        q.reshape(-1, L),
        m.reshape(-1, L),
        w,
        heat,
        plist,
        tally,
        loan,
        mate,
    )
    return (*out[:3], out[3][0, :1], out[4][0, :1])


def solution(mesh):
    return jax.shard_map(
        on_device,
        mesh=mesh,
        in_specs=(
            P("replica", None, "domain"),
            P("replica", None, "domain"),
            P("domain"),
            P("domain"),
            P("replica", None, None, "domain"),
            P("replica"),
            P("replica", "domain", None),
            P("replica", "domain"),
            P("replica", None, "domain"),
            P(),
        ),
        out_specs=(
            P("replica", None, "domain"),
            P("replica", None, "domain"),
            P("replica", None, "domain"),
            P("replica"),
            P("replica"),
        ),
        check_vma=False,
    )
```

```python
import functools
import math

import jax
import jax.numpy as jnp
from jax import lax
from jax.experimental import pallas as pl
from jax.experimental.pallas import tpu as pltpu
from jax.sharding import PartitionSpec as P

SLAB_LEN = 2.0
CUT_SQ = 9.0
FIELD_TERM = 1.0 / 54.0
HALF_STEP = 0.05
FRICTION_DECAY = math.exp(-0.5)
NOISE_SCALE = math.sqrt(1.0 - math.exp(-1.0))
KAPPA = 2.0 ** (1.0 / 3.0)
UNIT = KAPPA**-0.5
A = 3.0 / math.sqrt(2.0)
CHARGE_UNIT = math.sqrt(2.0) * KAPPA / 6.0
FORCE_UNIT = -2.0 / 243.0
ENERGY_UNIT = 0.5 * (KAPPA / 9.0) ** 2
FAR = 1.0e6
MESH = pl.DeviceIdType.MESH
L = 128
W = 8


def looked_up_early(groups):
    return (3 * groups) // 4


def picked(x, lane):
    return jnp.take_along_axis(x, lane, axis=1, mode="promise_in_bounds")


def fori(n, body, unroll=1):
    def step(i, c):
        body(i)
        return c

    lax.fori_loop(0, n, step, 0, unroll=unroll)


def wide(row):
    return jnp.broadcast_to(row, (W, L))


def kernel(
    replicas,
    domains,
    x_in,
    v_in,
    q_in,
    m_in,
    w_in,
    heat,
    plist_in,
    tally_in,
    loan_in,
    mate,
    x_out,
    v_out,
    f_out,
    pot_out,
    gap_out,
    own,
    halo,
    sbuf,
    qown,
    qhalo,
    qsend,
    vel,
    frc,
    rows,
    hm,
    nzc,
    noise,
    lane_ref,
    chunk_ref,
    self_ref,
    slane,
    schunk,
    part,
    qpart,
    eacc,
    epack,
    ebuf,
    rpack,
    rbuf,
    send_sem,
    recv_sem,
    qsend_sem,
    qrecv_sem,
    esend_sem,
    erecv_sem,
    rsend_sem,
    rrecv_sem,
):
    groups = own.shape[1]
    lent = sbuf.shape[2]
    partners = lane_ref.shape[1]
    steps = w_in.shape[2]
    early = looked_up_early(groups)
    me_r = lax.axis_index("replica")
    me_d = lax.axis_index("domain")
    nxt = lax.rem(me_d + 1, domains)
    prv = lax.rem(me_d + domains - 1, domains)
    box = SLAB_LEN * domains

    barrier = pltpu.get_barrier_semaphore()
    for o in range(1, domains):
        pl.semaphore_signal(
            barrier, inc=1, device_id=(me_r, lax.rem(me_d + o, domains)), device_id_type=MESH
        )
    for o in range(1, replicas):
        pl.semaphore_signal(
            barrier, inc=1, device_id=(lax.rem(me_r + o, replicas), me_d), device_id_type=MESH
        )

    sub_iota = lax.broadcasted_iota(jnp.int32, (W, L), 0)
    lane_iota = lax.broadcasted_iota(jnp.int32, (W, L), 1)
    in_lane = (lane_iota & 15) * W + sub_iota
    in_row = lane_iota >> 4
    out_lane = sub_iota * 16 + (lane_iota >> 3)
    out_row = lane_iota & 7

    def pack(row_of):
        acc = picked(wide(row_of(0)), in_lane)
        for r in range(1, W):
            acc = jnp.where(in_row == r, picked(wide(row_of(r)), in_lane), acc)
        return acc

    def unpack(ref, g, base):
        ref = ref.at[g]
        acc = picked(wide(ref[pl.ds(base, 1), :]), out_lane)
        for r in range(1, W):
            acc = jnp.where(out_row == r, picked(wide(ref[pl.ds(base + r, 1), :]), out_lane), acc)
        return acc

    kt = heat[0]

    def setup_coords(g):
        def at(r):
            return pl.ds(pl.multiple_of((g * W + r) * L, L), L)

        for f in range(3):
            own[0, g, f * W : (f + 1) * W, :] = UNIT * pack(lambda r: x_in[f, 0:1, at(r)])
        qown[g] = pack(lambda r: q_in[pl.ds(g * W + r, 1), :])

    fori(groups, setup_coords)

    def setup_loan(h):
        at = pl.ds(pl.multiple_of(h * L, L), L)
        for s in range(2):
            p = wide(loan_in[0, s : s + 1, at])
            slane[s, h] = p & (L - 1)
            schunk[s, h] = p >> 7

    fori(lent, setup_loan)

    def fill_send(s, slot):
        shift = jnp.where(
            me_d == (domains - 1 if s == 0 else 0), -box * UNIT if s == 0 else box * UNIT, 0.0
        ).astype(jnp.float32)

        def one(h):
            lane, chunk = slane[s, h], schunk[s, h]
            acc = [picked(own[slot, 0, f * W : (f + 1) * W, :], lane) for f in range(3)]
            for j in range(1, groups):
                hit = chunk == j
                for f in range(3):
                    acc[f] = jnp.where(hit, picked(own[slot, j, f * W : (f + 1) * W, :], lane), acc[f])
            acc[0] = acc[0] + shift
            for f in range(3):
                sbuf[slot, s, h, f * W : (f + 1) * W, :] = acc[f]

        fori(lent, one)

    def halo_copy(s, slot):
        return pltpu.make_async_remote_copy(
            src_ref=sbuf.at[slot, s],
            dst_ref=halo.at[slot, s],
            send_sem=send_sem.at[slot, s],
            recv_sem=recv_sem.at[slot, s],
            device_id=(me_r, nxt if s == 0 else prv),
            device_id_type=MESH,
        )

    def charge_copy(s):
        return pltpu.make_async_remote_copy(
            src_ref=qsend.at[s],
            dst_ref=qhalo.at[s],
            send_sem=qsend_sem.at[s],
            recv_sem=qrecv_sem.at[s],
            device_id=(me_r, nxt if s == 0 else prv),
            device_id_type=MESH,
        )

    def fill_charges(h):
        for s in range(2):
            lane, chunk = slane[s, h], schunk[s, h]
            acc = picked(qown[0], lane)
            for j in range(1, groups):
                acc = jnp.where(chunk == j, picked(qown[j], lane), acc)
            qsend[s, h] = acc

    fori(lent, fill_charges)
    pl.semaphore_wait(barrier, domains - 1 + replicas - 1)
    for s in range(2):
        charge_copy(s).start()

    def setup_lists(g):
        at = pl.ds(pl.multiple_of(g * L, L), L)
        p = plist_in[0, :, at]
        live = lax.broadcasted_iota(jnp.int32, p.shape, 0) < tally_in[0:1, at]
        lane_ref[g] = p & (L - 1)
        chunk_ref[g] = jnp.where(live, p >> 7, -1)
        here = g * L + lax.broadcasted_iota(jnp.int32, p.shape, 1)
        self_ref[g] = (p == here).astype(jnp.int32)

    def setup_rest(g):
        def at(r):
            return pl.ds(pl.multiple_of((g * W + r) * L, L), L)

        for f in range(3):
            vel[g, f * W : (f + 1) * W, :] = pack(lambda r: v_in[f, 0:1, at(r)])
        m = pack(lambda r: m_in[pl.ds(g * W + r, 1), :])
        hm[g] = (HALF_STEP * FORCE_UNIT) * m
        nzc[g] = NOISE_SCALE * jnp.sqrt(kt * m)

    def charges_near(g):
        for k in range(partners):
            lane, chunk = wide(lane_ref[g, k : k + 1, :]), wide(chunk_ref[g, k : k + 1, :])
            acc = jnp.zeros((W, L), jnp.float32)
            for j in range(groups):
                acc = jnp.where(chunk == j, picked(qown[j], lane), acc)
            qpart[g, k] = acc

    def charges_far(g):
        for k in range(partners):
            lane, chunk = wide(lane_ref[g, k : k + 1, :]), wide(chunk_ref[g, k : k + 1, :])
            acc = qpart[g, k]
            for s in range(2):
                for j in range(lent):
                    hit = chunk == groups + s * lent + j
                    acc = jnp.where(hit, picked(qhalo[s, j], lane), acc)
            qpart[g, k] = acc

    def near(slot):
        def one(g):
            for k in range(partners):
                lane, chunk = wide(lane_ref[g, k : k + 1, :]), wide(chunk_ref[g, k : k + 1, :])
                acc = [jnp.full((W, L), FAR, jnp.float32)] * 3
                for j in range(early):
                    hit = chunk == j
                    for f in range(3):
                        at = slice(f * W, (f + 1) * W)
                        acc[f] = jnp.where(hit, picked(own[slot, j, at, :], lane), acc[f])
                for f in range(3):
                    part[g, k, f * W : (f + 1) * W, :] = acc[f]

        fori(groups, one)

    def late(g, k, slot):
        lane, chunk = wide(lane_ref[g, pl.ds(k, 1), :]), wide(chunk_ref[g, pl.ds(k, 1), :])
        acc = [part[g, k, f * W : (f + 1) * W, :] for f in range(3)]
        for j in range(early, groups + 2 * lent):
            hit = chunk == j
            for f in range(3):
                at = slice(f * W, (f + 1) * W)
                if j < groups:
                    block = own[slot, j, at, :]
                else:
                    block = halo[slot, (j - groups) // lent, (j - groups) % lent, at, :]
                acc[f] = jnp.where(hit, picked(block, lane), acc[f])
        return acc

    def store_part(g, k, acc):
        for f in range(3):
            part[g, k, f * W : (f + 1) * W, :] = acc[f]

    per = partners // W

    def increments(f, n, at):
        row = w_in[0, f, 0:1, at]
        for step in range(1, steps):
            row = jnp.where(n == step, w_in[0, f, step : step + 1, at], row)
        return row

    def pairs(g, slot, n, with_energy):
        after = jnp.minimum(g + 1, groups - 1)

        def one_atom(i):
            ahead = [late(after, i * per + o, slot) for o in range(per)]
            if not with_energy:
                at = pl.ds(pl.multiple_of((g * W + i) * L, L), L)
                drawn = [
                    jnp.where(
                        in_row == i,
                        picked(wide(increments(f, n, at)), in_lane),
                        noise[f * W : (f + 1) * W, :],
                    )
                    for f in range(3)
                ]
            mine = [wide(own[slot, g, pl.ds(f * W + i, 1), :]) for f in range(3)]
            my_q = CHARGE_UNIT * wide(qown[g, pl.ds(i, 1), :])
            acc = [jnp.zeros((W, L), jnp.float32)] * 3
            energy = jnp.zeros((W, L), jnp.float32)
            for k in range(partners):
                d = [mine[f] - part[g, k, f * W : (f + 1) * W, :] for f in range(3)]
                t = d[0] * d[0] + d[1] * d[1] + d[2] * d[2]
                root = lax.rsqrt(t + 1.0 / KAPPA)
                inv = root * root
                p = inv * inv * inv
                y = (90.0 / (KAPPA * math.sqrt(2.0))) * inv
                q = my_q * qpart[g, k]
                w = jnp.maximum(CUT_SQ / KAPPA - t, 0.0)
                slope = w * (
                    p * (A + (y - 2.0 * A) * (1.0 - p))
                    + q * ((3.0 / KAPPA - t) - root * (y + 9.0 * A))
                )
                for f in range(3):
                    acc[f] = acc[f] + slope * d[f]
                if with_energy:
                    u = 0.25 * p * (p - 2.0) + q * (
                        (1.0 / (math.sqrt(KAPPA) * CHARGE_UNIT)) * root
                        + (KAPPA * FIELD_TERM / CHARGE_UNIT) * t
                    )
                    same = (sub_iota == i) & (wide(self_ref[g, k : k + 1, :]) == 1)
                    energy = energy + jnp.where(same, 0.0, u * (w * w))
            total = [jnp.sum(acc[f], axis=0, keepdims=True) for f in range(3)]
            for f in range(3):
                rows[pl.ds(f * W + i, 1), :] = total[f]
            if with_energy:
                eacc[...] += energy
            else:
                for f in range(3):
                    noise[f * W : (f + 1) * W, :] = drawn[f]
            for o in range(per):
                store_part(after, i * per + o, ahead[o])

        fori(W, one_atom, 8)

    def first_group(slot):
        fori(partners, lambda k: store_part(0, k, late(0, k, slot)))

    def exchange_start(slot):
        for s in range(2):
            fill_send(s, slot)
            halo_copy(s, slot).start()

    def exchange_wait(slot):
        for s in range(2):
            halo_copy(s, slot).wait()

    def step(n):
        slot = lax.rem(n, 2)
        then = 1 - slot
        near(slot)
        exchange_wait(slot)
        first_group(slot)
        kick = jnp.where(n == 0, 1.0, 2.0).astype(jnp.float32)

        def one(g):
            pairs(g, slot, n, False)
            for f in range(3):
                at = slice(f * W, (f + 1) * W)
                v = vel[g, at, :] + kick * (hm[g] * rows[at, :])
                x = own[slot, g, at, :] + (HALF_STEP * UNIT) * v
                v = FRICTION_DECAY * v + nzc[g] * noise[at, :]
                vel[g, at, :] = v
                own[then, g, at, :] = x + (HALF_STEP * UNIT) * v

        fori(groups, one)
        exchange_start(then)

    exchange_start(0)
    noise[...] = jnp.zeros_like(noise)
    fori(groups, setup_lists)
    fori(groups, setup_rest)
    fori(groups, charges_near)
    for s in range(2):
        charge_copy(s).wait()
    fori(groups, charges_far)
    fori(steps, step)

    last = steps % 2
    near(last)

    def store_out(g, ref, scale, out):
        for f in range(3):
            val = scale * unpack(ref, g, f * W)
            for r in range(W):
                at = pl.ds(pl.multiple_of((g * W + r) * L, L), L)
                out[f, 0:1, at] = val[r : r + 1, :]

    fori(groups, lambda g: store_out(g, own.at[last], 1.0 / UNIT, x_out))
    exchange_wait(last)
    first_group(last)
    eacc[...] = jnp.zeros_like(eacc)

    def final(g):
        pairs(g, last, 0, True)
        for f in range(3):
            at = slice(f * W, (f + 1) * W)
            frc[g, at, :] = rows[at, :]
            vel[g, at, :] = vel[g, at, :] + hm[g] * rows[at, :]

    fori(groups, final)

    epack[...] = jnp.full(epack.shape, ENERGY_UNIT * jnp.sum(eacc[...]), jnp.float32)

    def energy_copy(o):
        return pltpu.make_async_remote_copy(
            src_ref=epack,
            dst_ref=ebuf.at[me_d],
            send_sem=esend_sem.at[o],
            recv_sem=erecv_sem.at[o],
            device_id=(me_r, lax.rem(me_d + o, domains)),
            device_id_type=MESH,
        )

    for o in range(1, domains):
        energy_copy(o).start()
    ebuf[me_d] = epack[...]
    fori(groups, lambda g: store_out(g, frc, FORCE_UNIT, f_out))
    for o in range(1, domains):
        energy_copy(o).wait()
    total = ebuf[0]
    for d in range(1, domains):
        total = total + ebuf[d]
    per_atom = total / float(groups * L * W * domains)
    packet_lane = lax.broadcasted_iota(jnp.int32, per_atom.shape, 1)
    rpack[...] = jnp.where(packet_lane == 0, per_atom, kt)

    def rung_copy(o):
        return pltpu.make_async_remote_copy(
            src_ref=rpack,
            dst_ref=rbuf.at[me_r],
            send_sem=rsend_sem.at[o],
            recv_sem=rrecv_sem.at[o],
            device_id=(lax.rem(me_r + o, replicas), me_d),
            device_id_type=MESH,
        )

    for o in range(1, replicas):
        rung_copy(o).start()
    rbuf[me_r] = rpack[...]
    fori(groups, lambda g: store_out(g, vel, 1.0, v_out))
    for o in range(1, replicas):
        rung_copy(o).wait()
    partner = mate[0]
    for r in range(1, replicas):
        partner = jnp.where(me_r == r, mate[r], partner)
    other = rbuf[0]
    for r in range(1, replicas):
        other = jnp.where(partner == r, rbuf[r], other)
    other_e = jnp.sum(jnp.where(packet_lane == 0, other, 0.0))
    other_t = jnp.sum(jnp.where(packet_lane == 1, other, 0.0))
    gap = (1.0 / jnp.full_like(per_atom, kt) - 1.0 / jnp.full_like(per_atom, other_t)) * (
        per_atom - other_e
    )
    pot_out[...] = per_atom
    gap_out[...] = gap


def on_device(x, v, q, m, w, heat, plist, tally, loan, mate):
    replicas = lax.axis_size("replica")
    domains = lax.axis_size("domain")
    clusters, partners = plist.shape[1:]
    groups = clusters // L
    lent = loan.shape[2] // L
    f32, i32 = jnp.float32, jnp.int32
    state = (x.shape[1], 1, x.shape[2])
    vmem = pl.BlockSpec(memory_space=pltpu.VMEM)
    smem = pl.BlockSpec(memory_space=pltpu.SMEM)
    out = pl.pallas_call(
        functools.partial(kernel, replicas, domains),
        name="langevin",
        out_shape=(
            jax.ShapeDtypeStruct(state, f32),
            jax.ShapeDtypeStruct(state, f32),
            jax.ShapeDtypeStruct(state, f32),
            jax.ShapeDtypeStruct((1, L), f32),
            jax.ShapeDtypeStruct((1, L), f32),
        ),
        in_specs=[vmem, vmem, vmem, vmem, vmem, smem, vmem, vmem, vmem, smem],
        out_specs=(vmem,) * 5,
        scratch_shapes=[
            pltpu.VMEM((2, groups, 3 * W, L), f32),
            pltpu.VMEM((2, 2, lent, 3 * W, L), f32),
            pltpu.VMEM((2, 2, lent, 3 * W, L), f32),
            pltpu.VMEM((groups, W, L), f32),
            pltpu.VMEM((2, lent, W, L), f32),
            pltpu.VMEM((2, lent, W, L), f32),
            pltpu.VMEM((groups, 3 * W, L), f32),
            pltpu.VMEM((groups, 3 * W, L), f32),
            pltpu.VMEM((3 * W, L), f32),
            pltpu.VMEM((groups, W, L), f32),
            pltpu.VMEM((groups, W, L), f32),
            pltpu.VMEM((3 * W, L), f32),
            pltpu.VMEM((groups, partners, L), i32),
            pltpu.VMEM((groups, partners, L), i32),
            pltpu.VMEM((groups, partners, L), i32),
            pltpu.VMEM((2, lent, W, L), i32),
            pltpu.VMEM((2, lent, W, L), i32),
            pltpu.VMEM((groups, partners, 3 * W, L), f32),
            pltpu.VMEM((groups, partners, W, L), f32),
            pltpu.VMEM((W, L), f32),
            pltpu.VMEM((1, L), f32),
            pltpu.VMEM((domains, 1, L), f32),
            pltpu.VMEM((1, L), f32),
            pltpu.VMEM((replicas, 1, L), f32),
            pltpu.SemaphoreType.DMA((2, 2)),
            pltpu.SemaphoreType.DMA((2, 2)),
            pltpu.SemaphoreType.DMA((2,)),
            pltpu.SemaphoreType.DMA((2,)),
            pltpu.SemaphoreType.DMA((domains,)),
            pltpu.SemaphoreType.DMA((domains,)),
            pltpu.SemaphoreType.DMA((replicas,)),
            pltpu.SemaphoreType.DMA((replicas,)),
        ],
        compiler_params=pltpu.CompilerParams(collective_id=0, has_side_effects=True),
    )(
        x.transpose(1, 0, 2),
        v.transpose(1, 0, 2),
        q.reshape(-1, L),
        m.reshape(-1, L),
        w.transpose(0, 2, 1, 3),
        heat,
        plist.transpose(0, 2, 1),
        tally,
        loan,
        mate,
    )
    return (*(o.transpose(1, 0, 2) for o in out[:3]), out[3][0, :1], out[4][0, :1])


def solution(mesh):
    return jax.shard_map(
        on_device,
        mesh=mesh,
        in_specs=(
            P("replica", None, "domain"),
            P("replica", None, "domain"),
            P("domain"),
            P("domain"),
            P("replica", None, None, "domain"),
            P("replica"),
            P("replica", "domain", None),
            P("replica", "domain"),
            P("replica", None, "domain"),
            P(),
        ),
        out_specs=(
            P("replica", None, "domain"),
            P("replica", None, "domain"),
            P("replica", None, "domain"),
            P("replica"),
            P("replica"),
        ),
        check_vma=False,
    )
```
